32 devices in a mesh: dom: 8 (over y, x, core), sub: 4 (over z).
Axes of the slice: x: 2, y: 2, z: 4, core: 2. Of those that a mesh axis runs over, the one named last changes fastest.
Arguments:
- upstream: bfloat16 [65536, 128], P(('dom', 'sub')), may hold values from -6 to 6
- features: bfloat16 [65536, 128], P(('dom', 'sub')), may hold values from -6 to 6
- w_in: bfloat16 [128, 128], replicated, may hold values from -0.5 to 0.5
- w_out: bfloat16 [128, 128], replicated, may hold values from -0.5 to 0.5
- inner_adj: bfloat16 [65536, 2048], P(('dom', 'sub')), may hold values from -0.125 to 0.125
- cut_tiles: bfloat16 [768, 128, 128], P(('dom', 'sub')), may hold values from -0.15625 to 0.15625
- cut_list: int32 [768, 3], P(('dom', 'sub')), may hold values from 0 to 511, as said below
- cut_count: int32 [32], P(('dom', 'sub')), may hold values from 1 to 24, as said below
Outputs:
- input_grad: bfloat16 [65536, 128], P(('dom', 'sub'))
- grad_w_in: float32 [128, 128], replicated
- grad_w_out: float32 [128, 128], replicated
The draws below stay inside these ranges and needn't reach their ends.
Inputs may be any that keep to these rules, and one draw needn't show every extreme that they name: `cut_list`: device s's list has 24 rows; column 0 is a local block below 16, column 1 a global block whose device is not s, column 2 a tile id below 24, all tile ids of one device distinct. Among the first cut_count[s] rows the devices of column 1 are all distinct, so one device sends at most one block to another. `cut_count`: some device has exactly 24 live entries in every draw.
All inputs are finite; a program needn't handle non-finite values.
Results may differ from the reference program's by a relative error of at most 0.015.
Values may be sent and summed in bfloat16 or wider, within the bound.
A program may use at most 128 MiB of HBM per device.

```python
import math
import jax
import jax.numpy as jnp
from jax import lax

NB = 16
BLK = 128
EMB = 128
FEAT = 128
HID = 128
STEPS = 4
CMAX = 24
ROWS = 65536
N_DOM = 8
N_SUB = 4


def draw_cut_count(key, part):
    device_count = N_DOM * N_SUB
    key_base, key_heavy, key_pick = jax.random.split(jax.random.fold_in(key, 11), 3)
    base = jax.random.randint(key_base, (device_count,), 1, CMAX // 2 + 1)
    heavy = jax.random.randint(key_heavy, (device_count,), 0, 8) == 0
    picked = jax.random.randint(key_pick, (), 0, device_count)
    heavy = heavy | (jnp.arange(device_count) == picked)
    return jnp.where(heavy, CMAX, base).astype(jnp.int32)


def draw_cut_list(key, part):
    device_count = N_DOM * N_SUB
    list_key = jax.random.fold_in(key, 23)

    def draw_device(device):
        device_key = jax.random.fold_in(list_key, device)
        key_perm, key_target, key_read, key_tile = jax.random.split(device_key, 4)
        shuffled = jax.random.permutation(key_perm, device_count - 1)
        others = shuffled + (shuffled >= device).astype(shuffled.dtype)
        target_dev = others[:CMAX]
        target_block = target_dev * NB + jax.random.randint(key_target, (CMAX,), 0, NB)
        read_block = jax.random.randint(key_read, (CMAX,), 0, NB)
        tile_ids = jax.random.permutation(key_tile, CMAX)
        return jnp.stack([read_block.astype(jnp.int32), target_block.astype(jnp.int32), tile_ids.astype(jnp.int32)], 1)
    stacked = jax.vmap(draw_device)(jnp.arange(device_count, dtype=jnp.int32))
    return stacked.reshape(device_count * CMAX, 3).astype(jnp.int32)


def block_scale(rng, shape, cuts, smallest, top_value):
    def one(dim, blocks):
        steps = jax.random.uniform(jax.random.fold_in(jax.random.fold_in(rng, 6), dim), (blocks,), jnp.float32, smallest / len(cuts), top_value / len(cuts))
        return jnp.repeat(jnp.exp(steps), shape[dim] // blocks).reshape((-1,) + (1,) * (len(shape) - dim - 1))

    loudness = one(*cuts[0])
    for cut in cuts[1:]:
        loudness = loudness * one(*cut)
    return loudness


def noise(stream_key, extent, width, reach, cuts=(), kind=jnp.bfloat16):
    factor_of = block_scale(stream_key, extent, cuts, -0.22, 0.18) if cuts else 1.0
    values = jax.random.normal(stream_key, extent, jnp.float32) * width * factor_of
    return jnp.minimum(jnp.maximum(values, -reach), reach).astype(kind)


def setup_inputs(seed: int = 0) -> dict:
    key_list = jax.random.split(jax.random.key(seed), 9)
    upstream = noise(key_list[0], (ROWS, EMB), 1.0, 6.0, ((0, 32),))
    features = noise(key_list[1], (ROWS, FEAT), 1.0, 6.0, ((0, 32),))
    w_in = noise(key_list[2], (FEAT, HID), FEAT ** -0.5, 0.5)
    w_out = noise(key_list[3], (HID, EMB), HID ** -0.5, 0.5)
    inner_adj = noise(key_list[4], (ROWS, NB * BLK), (NB * BLK) ** -0.5, 0.125, ((0, 32),))
    cut_tiles = noise(key_list[5], (N_DOM * N_SUB * CMAX, BLK, BLK), (BLK * CMAX // 2) ** -0.5, 0.15625, ((0, 32),))
    cut_list = draw_cut_list(jax.random.fold_in(key_list[8], 71), 0)
    cut_count = draw_cut_count(jax.random.fold_in(key_list[8], 71), 0)
    return dict(upstream=upstream, features=features, w_in=w_in, w_out=w_out, inner_adj=inner_adj, cut_tiles=cut_tiles, cut_list=cut_list, cut_count=cut_count)


teleport = 0.1

def reference(upstream, features, w_in, w_out, inner_adj, cut_tiles, cut_list, cut_count):
    device_count = N_DOM * N_SUB
    local_rows = NB * BLK
    total_rows = local_rows * device_count
    adj_blocks = inner_adj.reshape(device_count, local_rows, local_rows)
    tile_sets = cut_tiles.reshape(device_count, CMAX, BLK, BLK)
    list_sets = cut_list.reshape(device_count, CMAX, 3)
    positions = jnp.arange(CMAX, dtype=jnp.int32)

    def local_product(pair):
        return jnp.dot(pair[0], pair[1], preferred_element_type=jnp.float32)

    def propagate(vector):
        parts = vector.reshape(device_count, local_rows, EMB)
        local_terms = lax.map(local_product, (adj_blocks, parts))
        blocks = parts.reshape(device_count, NB, BLK, EMB)

        def sender(carry, inputs):
            tiles_here, list_here, count_here, blocks_here = inputs
            chosen_tiles = tiles_here[list_here[:, 2].astype(jnp.int32)].astype(jnp.float32)
            chosen_blocks = blocks_here[list_here[:, 0].astype(jnp.int32)].astype(jnp.float32)
            products = jnp.einsum('cij,cjk->cik', chosen_tiles, chosen_blocks)
            products = jnp.where((positions < count_here)[:, None, None], products, jnp.zeros_like(products))
            rounded = lax.optimization_barrier(products.astype(jnp.bfloat16))
            carry = carry.at[list_here[:, 1].astype(jnp.int32)].add(rounded.astype(jnp.float32))
            return (carry, None)
        start_sum = jnp.zeros((device_count * NB, BLK, EMB), jnp.float32)
        cut_total, _ = lax.scan(sender, start_sum, (tile_sets, list_sets, cut_count, blocks))
        summed = local_terms.reshape(total_rows, EMB) + cut_total.reshape(total_rows, EMB)
        return ((1.0 - teleport) * summed).astype(jnp.bfloat16)
    vector = upstream
    accum = jnp.zeros((total_rows, EMB), jnp.float32)
    for section_index in range(STEPS):
        accum = accum + teleport * vector.astype(jnp.float32)
        vector = propagate(vector)
    head_grad = (accum + vector.astype(jnp.float32)).astype(jnp.bfloat16)
    pre = jnp.dot(features, w_in, preferred_element_type=jnp.float32)
    gate = jax.nn.sigmoid(pre)
    act = (pre * gate).astype(jnp.bfloat16)
    norm_scale = 1.0 / math.sqrt(total_rows)
    grad_w_out = jnp.einsum('rh,re->he', act.astype(jnp.float32), head_grad.astype(jnp.float32)) * norm_scale
    back = jnp.dot(head_grad, w_out.T, preferred_element_type=jnp.float32)
    dpre = (back * gate * (1.0 + pre * (1.0 - gate))).astype(jnp.bfloat16)
    grad_w_in = jnp.einsum('rf,rh->fh', features.astype(jnp.float32), dpre.astype(jnp.float32)) * norm_scale
    input_grad = jnp.dot(dpre, w_in.T, preferred_element_type=jnp.float32).astype(jnp.bfloat16)
    return (input_grad, grad_w_in, grad_w_out)
```

```python
import functools
import math

import jax
import jax.numpy as jnp
from jax import lax
from jax.experimental import pallas as pl
from jax.experimental.pallas import tpu as pltpu
from jax.sharding import PartitionSpec as P

STEPS = 4
teleport = 0.1
MESH = pl.DeviceIdType.MESH
F32 = jnp.float32
BF16 = jnp.bfloat16


def nt_dot(a, b):
    return lax.dot_general(a, b, (((1,), (1,)), ((), ())), preferred_element_type=F32)


def tn_dot(a, b):
    return lax.dot_general(a, b, (((0,), (0,)), ((), ())), preferred_element_type=F32)


def kernel(
    n_dom, n_sub, norm_scale,
    idx_ref, up_ref, tiles_ref, ids_out, w_in_ref, w_out_ref, adj_hbm, feat_hbm,
    ig_ref, gin_ref, gout_ref,
    adj, feat, v, outb, arrived, ids_in, acc, accum, fac, act, dpre, gsend, gparts, gred, gfull,
    local_sem, send_sem, recv_sem, id_send, id_recv,
):
    n = n_dom * n_sub
    my_dom, my_sub = lax.axis_index("dom"), lax.axis_index("sub")
    me = my_dom * n_sub + my_sub
    nb, blk, width = up_ref.shape
    rows = nb * blk
    tile = min(512, rows)
    blocks = tile // blk
    far = sorted(range(n_sub), key=lambda d: -min(d, n_sub - d))

    def peer(dz, i):
        d = lax.rem(my_dom + i, n_dom)
        z = lax.rem(my_sub + dz, n_sub)
        return d, z, d * n_sub + z

    def each_peer(fn):
        for dz in far:
            def body(i, carry, dz=dz):
                fn(*peer(dz, i))
                return carry
            lax.fori_loop(1 if dz == 0 else 0, n_dom, body, 0)

    adj_copy = pltpu.make_async_copy(adj_hbm, adj, local_sem.at[0])
    feat_copy = pltpu.make_async_copy(feat_hbm, feat, local_sem.at[1])
    adj_copy.start()
    feat_copy.start()

    barrier = pltpu.get_barrier_semaphore()
    each_peer(lambda d, z, t: pl.semaphore_signal(
        barrier, inc=1, device_id=(d, z), device_id_type=MESH))
    pl.semaphore_wait(barrier, n - 1)

    def id_copy(d, z, t, slot):
        return pltpu.make_async_remote_copy(
            src_ref=ids_out.at[t], dst_ref=ids_in.at[slot], send_sem=id_send.at[t],
            recv_sem=id_recv.at[slot], device_id=(d, z), device_id_type=MESH)

    def block_copy(p, d, z, t, slot):
        return pltpu.make_async_remote_copy(
            src_ref=outb.at[p, t], dst_ref=arrived.at[p, slot], send_sem=send_sem.at[p, t],
            recv_sem=recv_sem.at[p, slot], device_id=(d, z), device_id_type=MESH)

    each_peer(lambda d, z, t: id_copy(d, z, t, me).start())
    v[...] = up_ref[...]
    accum[...] = jnp.zeros_like(accum)

    for step in range(STEPS):
        p = step % 2

        def send(d, z, t):
            if step >= 2:
                block_copy(p, d, z, t, t).wait_send()
            product = jnp.dot(tiles_ref[idx_ref[1, t]], v[idx_ref[0, t]], preferred_element_type=F32)
            outb[p, t] = product.astype(BF16)
            block_copy(p, d, z, t, me).start()

        each_peer(send)

        if step == 0:
            feat_copy.wait()

            def head(i, carry):
                at = pl.ds(pl.multiple_of(i * tile, tile), tile)
                pre = jnp.dot(feat[at, :], w_in_ref[...], preferred_element_type=F32)
                gate = jax.nn.sigmoid(pre)
                act[at, :] = (pre * gate).astype(BF16)
                fac[at, :] = gate * (1.0 + pre * (1.0 - gate))
                return carry

            lax.fori_loop(0, rows // tile, head, 0)
            adj_copy.wait()

        def local(i, carry):
            at = pl.ds(pl.multiple_of(i * tile, tile), tile)
            term = jnp.dot(adj[at, :], v[...].reshape(rows, width), preferred_element_type=F32)
            ats = pl.ds(i * blocks, blocks)
            acc[ats] = term.reshape(blocks, blk, width)
            accum[ats] += teleport * v[ats].astype(F32)
            return carry

        lax.fori_loop(0, rows // tile, local, 0)

        for dz in reversed(far):
            first = 1 if dz == 0 else 0

            def arrive(i, carry):
                d, z, s = peer(dz, i)
                if step == 0:
                    id_copy(d, z, s, s).wait_recv()
                block_copy(p, d, z, s, s).wait_recv()
                return carry

            lax.fori_loop(first, n_dom, arrive, 0)

            def gather(b, carry):
                total = acc[b]
                for i in range(first, n_dom):
                    s = peer(dz, i)[2]
                    hit = ids_in[s][0:1, :] == b
                    total += jnp.where(hit, arrived[p, s].astype(F32), 0.0)
                acc[b] = total
                return carry

            lax.fori_loop(0, nb, gather, 0)

        def update(i, carry):
            ats = pl.ds(i * blocks, blocks)
            v[ats] = ((1.0 - teleport) * acc[ats]).astype(BF16)
            return carry

        lax.fori_loop(0, rows // tile, update, 0)

    def wait_sends(d, z, t):
        id_copy(d, z, t, t).wait_send()
        block_copy(0, d, z, t, t).wait_send()
        block_copy(1, d, z, t, t).wait_send()

    hid = w_in_ref.shape[1]
    feats = w_in_ref.shape[0]

    def tail(i, carry):
        part_in, part_out = carry
        at = pl.ds(pl.multiple_of(i * tile, tile), tile)
        ats = pl.ds(i * blocks, blocks)
        grad = (accum[ats] + v[ats].astype(F32)).astype(BF16).reshape(tile, width)
        part_out += tn_dot(act[at, :], grad)
        back = nt_dot(grad, w_out_ref[...])
        inner = (back * fac[at, :]).astype(BF16)
        dpre[at, :] = inner
        part_in += tn_dot(feat[at, :], inner)
        return part_in, part_out

    part_in, part_out = lax.fori_loop(
        0, rows // tile, tail,
        (jnp.zeros((feats, hid), F32), jnp.zeros((hid, width), F32)))
    chunk = gred.shape[0]
    owners = gsend.shape[0]
    gsend[0:feats // chunk] = (part_in * norm_scale).reshape(feats // chunk, chunk, hid)
    gsend[feats // chunk:owners] = (part_out * norm_scale).reshape(hid // chunk, chunk, width)
    each_peer(wait_sends)

    def part_copy(d, z, t, slot):
        return pltpu.make_async_remote_copy(
            src_ref=gsend.at[t], dst_ref=gparts.at[slot], send_sem=send_sem.at[0, t],
            recv_sem=recv_sem.at[0, slot], device_id=(d, z), device_id_type=MESH)

    def sum_copy(d, z, t, own, slot):
        return pltpu.make_async_remote_copy(
            src_ref=gred, dst_ref=gfull.at[own], send_sem=send_sem.at[1, t],
            recv_sem=recv_sem.at[1, slot], device_id=(d, z), device_id_type=MESH)

    def when_owner(t, fn):
        if owners == n:
            fn()
        else:
            pl.when(t < owners)(fn)

    each_peer(lambda d, z, t: when_owner(t, lambda: part_copy(d, z, t, me).start()))

    def input_grad(i, carry):
        at = pl.ds(pl.multiple_of(i * tile, tile), tile)
        ig_ref[at, :] = nt_dot(dpre[at, :], w_in_ref[...]).astype(BF16)
        return carry

    lax.fori_loop(0, rows // tile, input_grad, 0)

    def reduce():
        each_peer(lambda d, z, s: pltpu.make_async_remote_copy(
            src_ref=gsend.at[0], dst_ref=gparts.at[s], send_sem=send_sem.at[0, s],
            recv_sem=recv_sem.at[0, s], device_id=(d, z), device_id_type=MESH).wait_recv())
        gparts[me] = gsend[me]

        def add(i, total):
            return total + gparts[i]

        total = lax.fori_loop(1, n, add, gparts[0])
        gred[...] = total
        gfull[me] = total
        each_peer(lambda d, z, t: sum_copy(d, z, t, me, me).start())

    when_owner(me, reduce)
    each_peer(lambda d, z, t: when_owner(t, lambda: part_copy(d, z, t, t).wait_send()))
    each_peer(lambda d, z, s: when_owner(s, lambda: sum_copy(d, z, s, s, s).wait_recv()))
    when_owner(me, lambda: each_peer(lambda d, z, t: sum_copy(d, z, t, me, me).wait_send()))
    gin_ref[...] = gfull[0:feats // chunk].reshape(feats, hid)
    gout_ref[...] = gfull[feats // chunk:owners].reshape(hid, width)


def on_device(n_dom, n_sub, upstream, features, w_in, w_out, inner_adj, cut_tiles, cut_list, cut_count):
    n = n_dom * n_sub
    rows, width = upstream.shape
    entries, blk, _ = cut_tiles.shape
    nb = rows // blk
    feats, hid = w_in.shape
    live = jnp.arange(entries, dtype=jnp.int32) < cut_count[0]
    owner = cut_list[:, 1] // nb
    picked = (owner[None, :] == jnp.arange(n, dtype=jnp.int32)[:, None]) & live[None, :]
    pick = lambda x: jnp.sum(jnp.where(picked, x[None, :], 0), axis=1)
    idx = jnp.stack([pick(cut_list[:, 0]), pick(cut_list[:, 2])])
    block_id = nb + pick(cut_list[:, 1] % nb - nb)
    ids = jnp.broadcast_to(block_id[:, None, None], (n, 8, 128))
    grad_rows = feats + hid
    chunk = max(8, grad_rows // n)
    owners = grad_rows // chunk
    vmem = pl.BlockSpec(memory_space=pltpu.VMEM)
    hbm = pl.BlockSpec(memory_space=pl.ANY)
    scratch = [
        pltpu.VMEM(inner_adj.shape, BF16),
        pltpu.VMEM(features.shape, BF16),
        pltpu.VMEM((nb, blk, width), BF16),
        pltpu.VMEM((2, n, blk, width), BF16),
        pltpu.VMEM((2, n, blk, width), BF16),
        pltpu.VMEM((n, 8, 128), jnp.int32),
        pltpu.VMEM((nb, blk, width), F32),
        pltpu.VMEM((nb, blk, width), F32),
        pltpu.VMEM((rows, hid), F32),
        pltpu.VMEM((rows, hid), BF16),
        pltpu.VMEM((rows, hid), BF16),
        pltpu.VMEM((owners, chunk, hid), F32),
        pltpu.VMEM((n, chunk, hid), F32),
        pltpu.VMEM((chunk, hid), F32),
        pltpu.VMEM((owners, chunk, hid), F32),
        pltpu.SemaphoreType.DMA((2,)),
        pltpu.SemaphoreType.DMA((2, n)),
        pltpu.SemaphoreType.DMA((2, n)),
        pltpu.SemaphoreType.DMA((n,)),
        pltpu.SemaphoreType.DMA((n,)),
    ]
    return pl.pallas_call(
        functools.partial(kernel, n_dom, n_sub, 1.0 / math.sqrt(rows * n)),
        out_shape=(
            jax.ShapeDtypeStruct((rows, feats), BF16),
            jax.ShapeDtypeStruct((feats, hid), F32),
            jax.ShapeDtypeStruct((hid, width), F32),
        ),
        in_specs=[pl.BlockSpec(memory_space=pltpu.SMEM)] + [vmem] * 5 + [hbm] * 2,
        out_specs=(vmem, vmem, vmem),
        scratch_shapes=scratch,
        compiler_params=pltpu.CompilerParams(collective_id=0, has_side_effects=True),
    )(idx, upstream.reshape(nb, blk, width), cut_tiles, ids, w_in, w_out, inner_adj, features)


def solution(mesh):
    both = ("dom", "sub")
    placed = (
        P(both, None),
        P(both, None),
        P(),
        P(),
        P(both, None),
        P(both, None, None),
        P(both, None),
        P(both),
    )
    return jax.shard_map(
        functools.partial(on_device, mesh.shape["dom"], mesh.shape["sub"]),
        mesh=mesh,
        in_specs=placed,
        out_specs=(P(both, None), P(), P()),
        check_vma=False,
    )
```

```python
import functools
import math

import jax
import jax.numpy as jnp
from jax import lax
from jax.experimental import pallas as pl
from jax.experimental.pallas import tpu as pltpu
from jax.sharding import PartitionSpec as P

STEPS = 4
teleport = 0.1
MESH = pl.DeviceIdType.MESH
F32 = jnp.float32
BF16 = jnp.bfloat16


def nt_dot(a, b):
    return lax.dot_general(a, b, (((1,), (1,)), ((), ())), preferred_element_type=F32)


def tn_dot(a, b):
    return lax.dot_general(a, b, (((0,), (0,)), ((), ())), preferred_element_type=F32)


def kernel(
    n_dom, n_sub, norm_scale,
    idx_ref, up_ref, tiles_ref, ids_out, w_in_ref, w_out_ref, adj_hbm, feat_hbm,
    dpre, gfull,
    adj, feat, v, outb, arrived, ids_in, acc, accum, fac, act, gsend, gparts, gred,
    local_sem, send_sem, recv_sem, id_send, id_recv,
):
    n = n_dom * n_sub
    my_dom, my_sub = lax.axis_index("dom"), lax.axis_index("sub")
    me = my_dom * n_sub + my_sub
    nb, blk, width = up_ref.shape
    rows = nb * blk
    tile = min(512, rows)
    blocks = tile // blk
    paired = n_sub & (n_sub - 1) == 0
    pairings = list(reversed(range(n_sub)))
    arrivals = [(0, 1, n_dom)]
    for m in pairings[:-1]:
        arrivals += [(m, 0, n_dom // 2), (m, n_dom // 2, n_dom)]

    def partner(m, sign):
        if not paired:
            return lax.rem(my_sub + sign * m + n_sub, n_sub)
        z, bit = my_sub, 1
        while bit < n_sub:
            if m & bit:
                z = z + bit - 2 * bit * lax.rem(my_sub // bit, 2)
            bit *= 2
        return z

    def peer(m, i, sign=1):
        d = lax.rem(my_dom + sign * i + n_dom, n_dom)
        z = partner(m, sign)
        return d, z, d * n_sub + z

    def each_peer(fn):
        for m in pairings:
            def body(i, carry, m=m):
                fn(*peer(m, i))
                return carry
            lax.fori_loop(1 if m == 0 else 0, n_dom, body, 0)

    adj_copy = pltpu.make_async_copy(adj_hbm, adj, local_sem.at[0])
    feat_copy = pltpu.make_async_copy(feat_hbm, feat, local_sem.at[1])
    adj_copy.start()
    feat_copy.start()

    barrier = pltpu.get_barrier_semaphore()
    each_peer(lambda d, z, t: pl.semaphore_signal(
        barrier, inc=1, device_id=(d, z), device_id_type=MESH))
    pl.semaphore_wait(barrier, n - 1)

    def id_copy(d, z, t, slot):
        return pltpu.make_async_remote_copy(
            src_ref=ids_out.at[t, 0:1], dst_ref=ids_in.at[slot, 0:1], send_sem=id_send.at[t],
            recv_sem=id_recv.at[slot], device_id=(d, z), device_id_type=MESH)

    def block_copy(p, d, z, t, slot):
        return pltpu.make_async_remote_copy(
            src_ref=outb.at[p, t], dst_ref=arrived.at[p, slot], send_sem=send_sem.at[p, t],
            recv_sem=recv_sem.at[p, slot], device_id=(d, z), device_id_type=MESH)

    each_peer(lambda d, z, t: id_copy(d, z, t, me).start())
    v[...] = up_ref[...]
    accum[...] = jnp.zeros_like(accum)

    for step in range(STEPS):
        p = step % 2

        def send(d, z, t):
            if step >= 2:
                block_copy(p, d, z, t, t).wait_send()
            product = jnp.dot(tiles_ref[idx_ref[1, t]], v[idx_ref[0, t]], preferred_element_type=F32)
            outb[p, t] = product.astype(BF16)
            block_copy(p, d, z, t, me).start()

        each_peer(send)

        if step == 0:
            feat_copy.wait()

            def head(i, carry):
                at = pl.ds(pl.multiple_of(i * tile, tile), tile)
                pre = jnp.dot(feat[at, :], w_in_ref[...], preferred_element_type=F32)
                gate = jax.nn.sigmoid(pre)
                act[at, :] = (pre * gate).astype(BF16)
                fac[at, :] = gate * (1.0 + pre * (1.0 - gate))
                return carry

            lax.fori_loop(0, rows // tile, head, 0)
            adj_copy.wait()

        def local(i, carry):
            at = pl.ds(pl.multiple_of(i * tile, tile), tile)
            term = jnp.dot(adj[at, :], v[...].reshape(rows, width), preferred_element_type=F32)
            ats = pl.ds(i * blocks, blocks)
            acc[ats] = term.reshape(blocks, blk, width)
            accum[ats] += teleport * v[ats].astype(F32)
            return carry

        lax.fori_loop(0, rows // tile, local, 0)

        for m, first, end in arrivals:
            last = (m, first, end) == arrivals[-1]

            def arrive(i, carry):
                d, z, s = peer(m, i, -1)
                if step == 0:
                    id_copy(d, z, s, s).wait_recv()
                block_copy(p, d, z, s, s).wait_recv()
                return carry

            lax.fori_loop(first, end, arrive, 0)

            def gather(b, carry):
                total = acc[b]
                for i in range(first, end):
                    s = peer(m, i, -1)[2]
                    hit = ids_in[s, 0:1, :] == b
                    total += jnp.where(hit, arrived[p, s].astype(F32), 0.0)
                if last:
                    v[b] = ((1.0 - teleport) * total).astype(BF16)
                else:
                    acc[b] = total
                return carry

            lax.fori_loop(0, nb, gather, 0)

    def wait_sends(d, z, t):
        id_copy(d, z, t, t).wait_send()
        block_copy(0, d, z, t, t).wait_send()
        block_copy(1, d, z, t, t).wait_send()

    hid = w_in_ref.shape[1]
    feats = w_in_ref.shape[0]

    def tail(i, carry):
        part_in, part_out = carry
        at = pl.ds(pl.multiple_of(i * tile, tile), tile)
        ats = pl.ds(i * blocks, blocks)
        grad = (accum[ats] + v[ats].astype(F32)).astype(BF16).reshape(tile, width)
        part_out += tn_dot(act[at, :], grad)
        back = nt_dot(grad, w_out_ref[...])
        inner = (back * fac[at, :]).astype(BF16)
        dpre[at, :] = inner
        part_in += tn_dot(feat[at, :], inner)
        return part_in, part_out

    part_in, part_out = lax.fori_loop(
        0, rows // tile, tail,
        (jnp.zeros((feats, hid), F32), jnp.zeros((hid, width), F32)))
    chunk = gred.shape[0]
    owners = gsend.shape[0]
    gsend[0:feats // chunk] = (part_in * norm_scale).reshape(feats // chunk, chunk, hid).astype(BF16)
    gsend[feats // chunk:owners] = (part_out * norm_scale).reshape(hid // chunk, chunk, width).astype(BF16)
    each_peer(wait_sends)

    def part_copy(d, z, t, slot):
        return pltpu.make_async_remote_copy(
            src_ref=gsend.at[t], dst_ref=gparts.at[slot], send_sem=send_sem.at[0, t],
            recv_sem=recv_sem.at[0, slot], device_id=(d, z), device_id_type=MESH)

    def sum_copy(d, z, t, own, slot):
        return pltpu.make_async_remote_copy(
            src_ref=gred, dst_ref=gfull.at[own], send_sem=send_sem.at[1, t],
            recv_sem=recv_sem.at[1, slot], device_id=(d, z), device_id_type=MESH)

    def when_owner(t, fn):
        if owners == n:
            fn()
        else:
            pl.when(t < owners)(fn)

    each_peer(lambda d, z, t: when_owner(t, lambda: part_copy(d, z, t, me).start()))

    def reduce():
        each_peer(lambda d, z, s: pltpu.make_async_remote_copy(
            src_ref=gsend.at[0], dst_ref=gparts.at[s], send_sem=send_sem.at[0, s],
            recv_sem=recv_sem.at[0, s], device_id=(d, z), device_id_type=MESH).wait_recv())
        gparts[me] = gsend[me]

        def add(i, total):
            return total + gparts[i].astype(F32)

        total = lax.fori_loop(1, n, add, gparts[0].astype(F32)).astype(BF16)
        gred[...] = total
        gfull[me] = total
        each_peer(lambda d, z, t: sum_copy(d, z, t, me, me).start())

    when_owner(me, reduce)
    each_peer(lambda d, z, t: when_owner(t, lambda: part_copy(d, z, t, t).wait_send()))
    each_peer(lambda d, z, s: when_owner(s, lambda: sum_copy(d, z, s, s, s).wait_recv()))
    when_owner(me, lambda: each_peer(lambda d, z, t: sum_copy(d, z, t, me, me).wait_send()))


def finish(dpre_ref, w_in_ref, gfull_ref, ig_ref, gin_ref, gout_ref):
    owners, chunk, _ = gfull_ref.shape
    split = gin_ref.shape[0] // chunk
    ig_ref[...] = nt_dot(dpre_ref[...], w_in_ref[...]).astype(BF16)
    gin_ref[...] = gfull_ref[0:split].astype(F32).reshape(gin_ref.shape)
    gout_ref[...] = gfull_ref[split:owners].astype(F32).reshape(gout_ref.shape)


def on_device(n_dom, n_sub, upstream, features, w_in, w_out, inner_adj, cut_tiles, cut_list, cut_count):
    n = n_dom * n_sub
    rows, width = upstream.shape
    entries, blk, _ = cut_tiles.shape
    nb = rows // blk
    feats, hid = w_in.shape
    live = jnp.arange(entries, dtype=jnp.int32) < cut_count[0]
    owner = cut_list[:, 1] // nb
    picked = (owner[None, :] == jnp.arange(n, dtype=jnp.int32)[:, None]) & live[None, :]
    pick = lambda x: jnp.sum(jnp.where(picked, x[None, :], 0), axis=1)
    idx = jnp.stack([pick(cut_list[:, 0]), pick(cut_list[:, 2])])
    block_id = nb + pick(cut_list[:, 1] % nb - nb)
    ids = jnp.broadcast_to(block_id[:, None, None], (n, 8, 128))
    grad_rows = feats + hid
    chunk = max(8, grad_rows // n)
    owners = grad_rows // chunk
    vmem = pl.BlockSpec(memory_space=pltpu.VMEM)
    hbm = pl.BlockSpec(memory_space=pl.ANY)
    scratch = [
        pltpu.VMEM(inner_adj.shape, BF16),
        pltpu.VMEM(features.shape, BF16),
        pltpu.VMEM((nb, blk, width), BF16),
        pltpu.VMEM((2, n, blk, width), BF16),
        pltpu.VMEM((2, n, blk, width), BF16),
        pltpu.VMEM((n, 8, 128), jnp.int32),
        pltpu.VMEM((nb, blk, width), F32),
        pltpu.VMEM((nb, blk, width), F32),
        pltpu.VMEM((rows, hid), F32),
        pltpu.VMEM((rows, hid), BF16),
        pltpu.VMEM((owners, chunk, hid), BF16),
        pltpu.VMEM((n, chunk, hid), BF16),
        pltpu.VMEM((chunk, hid), BF16),
        pltpu.SemaphoreType.DMA((2,)),
        pltpu.SemaphoreType.DMA((2, n)),
        pltpu.SemaphoreType.DMA((2, n)),
        pltpu.SemaphoreType.DMA((n,)),
        pltpu.SemaphoreType.DMA((n,)),
    ]
    dpre, sums = pl.pallas_call(
        functools.partial(kernel, n_dom, n_sub, 1.0 / math.sqrt(rows * n)),
        out_shape=(
            jax.ShapeDtypeStruct((rows, hid), BF16),
            jax.ShapeDtypeStruct((owners, chunk, hid), BF16),
        ),
        in_specs=[pl.BlockSpec(memory_space=pltpu.SMEM)] + [vmem] * 5 + [hbm] * 2,
        out_specs=(vmem, vmem),
        scratch_shapes=scratch,
        compiler_params=pltpu.CompilerParams(collective_id=0, has_side_effects=True),
    )(idx, upstream.reshape(nb, blk, width), cut_tiles, ids, w_in, w_out, inner_adj, features)
    return pl.pallas_call(
        finish,
        out_shape=(
            jax.ShapeDtypeStruct((rows, feats), BF16),
            jax.ShapeDtypeStruct((feats, hid), F32),
            jax.ShapeDtypeStruct((hid, width), F32),
        ),
        in_specs=[vmem] * 3,
        out_specs=(vmem, vmem, vmem),
    )(dpre, w_in, sums)


def solution(mesh):
    both = ("dom", "sub")
    placed = (
        P(both, None),
        P(both, None),
        P(),
        P(),
        P(both, None),
        P(both, None, None),
        P(both, None),
        P(both),
    )
    return jax.shard_map(
        functools.partial(on_device, mesh.shape["dom"], mesh.shape["sub"]),
        mesh=mesh,
        in_specs=placed,
        out_specs=(P(both, None), P(), P()),
        check_vma=False,
    )
```

```python
import functools
import math

import jax
import jax.numpy as jnp
from jax import lax
from jax.experimental import pallas as pl
from jax.experimental.pallas import tpu as pltpu
from jax.sharding import PartitionSpec as P

STEPS = 4
teleport = 0.1
MESH = pl.DeviceIdType.MESH
F32 = jnp.float32
BF16 = jnp.bfloat16


def nt_dot(a, b):
    return lax.dot_general(a, b, (((1,), (1,)), ((), ())), preferred_element_type=F32)


def tn_dot(a, b):
    return lax.dot_general(a, b, (((0,), (0,)), ((), ())), preferred_element_type=F32)


def kernel(
    n_dom, n_sub, norm_scale,
    idx_ref, up_ref, tiles_ref, ids_out, w_in_ref, w_out_ref, adj_hbm, feat_hbm,
    dpre, gfull,
    adj, feat, v, outb, arrived, ids_in, acc, accum, fac, act, gsend, gparts, gred,
    local_sem, send_sem, recv_sem, id_send, id_recv,
):
    n = n_dom * n_sub
    my_dom, my_sub = lax.axis_index("dom"), lax.axis_index("sub")
    me = my_dom * n_sub + my_sub
    nb, blk, width = up_ref.shape
    rows = nb * blk
    tile = min(512, rows)
    blocks = tile // blk
    paired = n_sub & (n_sub - 1) == 0
    pairings = list(reversed(range(n_sub)))
    arrivals = [(0, 1, n_dom)]
    for m in pairings[:-1]:
        arrivals += [(m, i, min(i + 2, n_dom)) for i in range(0, n_dom, 2)] if m == 1 else [(m, 0, n_dom // 2), (m, n_dom // 2, n_dom)]

    def partner(m, sign):
        if not paired:
            return lax.rem(my_sub + sign * m + n_sub, n_sub)
        z, bit = my_sub, 1
        while bit < n_sub:
            if m & bit:
                z = z + bit - 2 * bit * lax.rem(my_sub // bit, 2)
            bit *= 2
        return z

    def peer(m, i, sign=1):
        d = lax.rem(my_dom + sign * i + n_dom, n_dom)
        z = partner(m, sign)
        return d, z, d * n_sub + z

    def each_peer(fn):
        for m in pairings:
            def body(i, carry, m=m):
                fn(*peer(m, i))
                return carry
            lax.fori_loop(1 if m == 0 else 0, n_dom, body, 0)

    adj_copy = pltpu.make_async_copy(adj_hbm, adj, local_sem.at[0])
    feat_copy = pltpu.make_async_copy(feat_hbm, feat, local_sem.at[1])
    adj_copy.start()
    feat_copy.start()

    barrier = pltpu.get_barrier_semaphore()
    each_peer(lambda d, z, t: pl.semaphore_signal(
        barrier, inc=1, device_id=(d, z), device_id_type=MESH))
    pl.semaphore_wait(barrier, n - 1)

    def id_copy(d, z, t, slot):
        return pltpu.make_async_remote_copy(
            src_ref=ids_out.at[t], dst_ref=ids_in.at[slot], send_sem=id_send.at[t],
            recv_sem=id_recv.at[slot], device_id=(d, z), device_id_type=MESH)

    def block_copy(p, d, z, t, slot):
        return pltpu.make_async_remote_copy(
            src_ref=outb.at[p, t], dst_ref=arrived.at[p, slot], send_sem=send_sem.at[p, t],
            recv_sem=recv_sem.at[p, slot], device_id=(d, z), device_id_type=MESH)

    each_peer(lambda d, z, t: id_copy(d, z, t, me).start())
    v[...] = up_ref[...]
    accum[...] = jnp.zeros_like(accum)

    for step in range(STEPS):
        p = step % 2

        def send(d, z, t):
            if step >= 2:
                block_copy(p, d, z, t, t).wait_send()
            product = jnp.dot(tiles_ref[idx_ref[2, t]], v[idx_ref[0, t]], preferred_element_type=F32)
            outb[p, t] = product.astype(BF16)
            block_copy(p, d, z, t, me).start()

        each_peer(send)

        if step == 0:
            feat_copy.wait()

            def head(i, carry):
                at = pl.ds(pl.multiple_of(i * tile, tile), tile)
                pre = jnp.dot(feat[at, :], w_in_ref[...], preferred_element_type=F32)
                gate = jax.nn.sigmoid(pre)
                act[at, :] = (pre * gate).astype(BF16)
                fac[at, :] = gate * (1.0 + pre * (1.0 - gate))
                return carry

            lax.fori_loop(0, rows // tile, head, 0)
            adj_copy.wait()

        def local(i, carry):
            at = pl.ds(pl.multiple_of(i * tile, tile), tile)
            term = jnp.dot(adj[at, :], v[...].reshape(rows, width), preferred_element_type=F32)
            ats = pl.ds(i * blocks, blocks)
            acc[ats] = term.reshape(blocks, blk, width)
            accum[ats] += teleport * v[ats].astype(F32)
            return carry

        lax.fori_loop(0, rows // tile, local, 0)

        for m, first, end in arrivals:
            last = (m, first, end) == arrivals[-1]

            def arrive(i, carry):
                d, z, s = peer(m, i, -1)
                if step == 0:
                    id_copy(d, z, s, s).wait_recv()
                block_copy(p, d, z, s, s).wait_recv()
                return carry

            lax.fori_loop(first, end, arrive, 0)

            def gather(b, carry):
                total = acc[b]
                for i in range(first, end):
                    s = peer(m, i, -1)[2]
                    hit = ids_in[s, 0:1, :] == b
                    total += jnp.where(hit, arrived[p, s].astype(F32), 0.0)
                if last:
                    v[b] = ((1.0 - teleport) * total).astype(BF16)
                else:
                    acc[b] = total
                return carry

            lax.fori_loop(0, nb, gather, 0, unroll=2)

    def wait_sends(d, z, t):
        id_copy(d, z, t, t).wait_send()
        block_copy(0, d, z, t, t).wait_send()
        block_copy(1, d, z, t, t).wait_send()

    hid = w_in_ref.shape[1]
    feats = w_in_ref.shape[0]

    def tail(i, carry):
        part_in, part_out = carry
        at = pl.ds(pl.multiple_of(i * tile, tile), tile)
        ats = pl.ds(i * blocks, blocks)
        grad = (accum[ats] + v[ats].astype(F32)).astype(BF16).reshape(tile, width)
        part_out += tn_dot(act[at, :], grad)
        back = nt_dot(grad, w_out_ref[...])
        inner = (back * fac[at, :]).astype(BF16)
        dpre[at, :] = inner
        part_in += tn_dot(feat[at, :], inner)
        return part_in, part_out

    part_in, part_out = lax.fori_loop(
        0, rows // tile, tail,
        (jnp.zeros((feats, hid), F32), jnp.zeros((hid, width), F32)))
    chunk = gred.shape[0]
    owners = gsend.shape[0]
    gsend[0:feats // chunk] = (part_in * norm_scale).reshape(feats // chunk, chunk, hid).astype(BF16)
    gsend[feats // chunk:owners] = (part_out * norm_scale).reshape(hid // chunk, chunk, width).astype(BF16)
    each_peer(wait_sends)

    def part_copy(d, z, t, slot):
        return pltpu.make_async_remote_copy(
            src_ref=gsend.at[t], dst_ref=gparts.at[slot], send_sem=send_sem.at[0, t],
            recv_sem=recv_sem.at[0, slot], device_id=(d, z), device_id_type=MESH)

    def sum_copy(d, z, t, own, slot):
        return pltpu.make_async_remote_copy(
            src_ref=gred, dst_ref=gfull.at[own], send_sem=send_sem.at[1, t],
            recv_sem=recv_sem.at[1, slot], device_id=(d, z), device_id_type=MESH)

    def when_owner(t, fn):
        if owners == n:
            fn()
        else:
            pl.when(t < owners)(fn)

    each_peer(lambda d, z, t: when_owner(t, lambda: part_copy(d, z, t, me).start()))

    def reduce():
        each_peer(lambda d, z, s: pltpu.make_async_remote_copy(
            src_ref=gsend.at[0], dst_ref=gparts.at[s], send_sem=send_sem.at[0, s],
            recv_sem=recv_sem.at[0, s], device_id=(d, z), device_id_type=MESH).wait_recv())
        gparts[me] = gsend[me]

        def add(i, total):
            return total + gparts[i].astype(F32)

        total = lax.fori_loop(1, n, add, gparts[0].astype(F32)).astype(BF16)
        gred[...] = total
        gfull[me] = total
        each_peer(lambda d, z, t: sum_copy(d, z, t, me, me).start())

    when_owner(me, reduce)
    each_peer(lambda d, z, t: when_owner(t, lambda: part_copy(d, z, t, t).wait_send()))
    each_peer(lambda d, z, s: when_owner(s, lambda: sum_copy(d, z, s, s, s).wait_recv()))
    when_owner(me, lambda: each_peer(lambda d, z, t: sum_copy(d, z, t, me, me).wait_send()))


def finish(dpre_ref, w_in_ref, gfull_ref, ig_ref, gin_ref, gout_ref):
    owners, chunk, _ = gfull_ref.shape
    split = gin_ref.shape[0] // chunk
    ig_ref[...] = nt_dot(dpre_ref[...], w_in_ref[...]).astype(BF16)
    gin_ref[...] = gfull_ref[0:split].astype(F32).reshape(gin_ref.shape)
    gout_ref[...] = gfull_ref[split:owners].astype(F32).reshape(gout_ref.shape)


def on_device(n_dom, n_sub, upstream, features, w_in, w_out, inner_adj, cut_tiles, cut_list, cut_count):
    n = n_dom * n_sub
    rows, width = upstream.shape
    entries, blk, _ = cut_tiles.shape
    nb = rows // blk
    feats, hid = w_in.shape
    live = jnp.arange(entries, dtype=jnp.int32) < cut_count[0]
    owner = jnp.where(live, cut_list[:, 1] // nb, n)
    picked = owner[None, :] == jnp.arange(n, dtype=jnp.int32)[:, None]
    idx = jnp.sum(jnp.where(picked[None], cut_list.T[:, None, :], 0), axis=2)
    block_id = jnp.where(jnp.any(picked, axis=1), idx[1] % nb, nb)
    ids = jnp.broadcast_to(block_id[:, None, None], (n, 1, 128))
    grad_rows = feats + hid
    chunk = max(8, grad_rows // n)
    owners = grad_rows // chunk
    vmem = pl.BlockSpec(memory_space=pltpu.VMEM)
    hbm = pl.BlockSpec(memory_space=pl.ANY)
    scratch = [
        pltpu.VMEM(inner_adj.shape, BF16),
        pltpu.VMEM(features.shape, BF16),
        pltpu.VMEM((nb, blk, width), BF16),
        pltpu.VMEM((2, n, blk, width), BF16),
        pltpu.VMEM((2, n, blk, width), BF16),
        pltpu.VMEM((n, 1, 128), jnp.int32),
        pltpu.VMEM((nb, blk, width), F32),
        pltpu.VMEM((nb, blk, width), F32),
        pltpu.VMEM((rows, hid), F32),
        pltpu.VMEM((rows, hid), BF16),
        pltpu.VMEM((owners, chunk, hid), BF16),
        pltpu.VMEM((n, chunk, hid), BF16),
        pltpu.VMEM((chunk, hid), BF16),
        pltpu.SemaphoreType.DMA((2,)),
        pltpu.SemaphoreType.DMA((2, n)),
        pltpu.SemaphoreType.DMA((2, n)),
        pltpu.SemaphoreType.DMA((n,)),
        pltpu.SemaphoreType.DMA((n,)),
    ]
    dpre, sums = pl.pallas_call(
        functools.partial(kernel, n_dom, n_sub, 1.0 / math.sqrt(rows * n)),
        out_shape=(
            jax.ShapeDtypeStruct((rows, hid), BF16),
            jax.ShapeDtypeStruct((owners, chunk, hid), BF16),
        ),
        in_specs=[pl.BlockSpec(memory_space=pltpu.SMEM)] + [vmem] * 5 + [hbm] * 2,
        out_specs=(vmem, vmem),
        scratch_shapes=scratch,
        compiler_params=pltpu.CompilerParams(collective_id=0, has_side_effects=True),
    )(idx, upstream.reshape(nb, blk, width), cut_tiles, ids, w_in, w_out, inner_adj, features)
    return pl.pallas_call(
        finish,
        out_shape=(
            jax.ShapeDtypeStruct((rows, feats), BF16),
            jax.ShapeDtypeStruct((feats, hid), F32),
            jax.ShapeDtypeStruct((hid, width), F32),
        ),
        in_specs=[vmem] * 3,
        out_specs=(vmem, vmem, vmem),
    )(dpre, w_in, sums)


def solution(mesh):
    both = ("dom", "sub")
    placed = (
        P(both, None),
        P(both, None),
        P(),
        P(),
        P(both, None),
        P(both, None, None),
        P(both, None),
        P(both),
    )
    return jax.shard_map(
        functools.partial(on_device, mesh.shape["dom"], mesh.shape["sub"]),
        mesh=mesh,
        in_specs=placed,
        out_specs=(P(both, None), P(), P()),
        check_vma=False,
    )
```
